32 devices in a mesh: grp: 2 (over x), res: 16 (over z, y, core).
Axes of the slice: x: 2, y: 2, z: 4, core: 2. Of those that a mesh axis runs over, the one named last changes fastest.
Arguments:
- stacked_sequence_embedding: bfloat16 [1024, 8192], P(('grp', 'res')), parts along dimension 0, may hold values from -6 to 6
- normalizer_multiplier: float32 [64], replicated, may hold values from 0.1 to 1.9
- normalizer_additive: float32 [64], replicated, may hold values from -2 to 2
- lhs_projected_tensor: bfloat16 [64, 32], replicated, may hold values from -0.75 to 0.75
- rhs_projected_tensor: bfloat16 [64, 32], replicated, may hold values from -0.75 to 0.75
- pairwise_matrix: bfloat16 [1024, 128], replicated, may hold values from -0.359375 to 0.359375
- pairwise_shift: float32 [128], replicated, may hold values from -3 to 3
Outputs:
- pair_update: bfloat16 [256, 128, 128], P(('grp', 'res')), parts along dimension 0
The draws below stay inside these ranges and needn't reach their ends.
There are 2 independent parts, one for each index of `grp`. The reference program is written for one: setup_inputs(seed, part) draws one part's arguments, and reference() takes and returns one part's arrays. A program takes and returns all parts, laid end to end along the dimension named above; an argument that names none is the same for every part. Nothing has to cross between parts.
All inputs are finite; a program needn't handle non-finite values.
Results may differ from the reference program's by a relative error of at most 0.0047.
Values may be sent and summed in bfloat16 or wider, within the bound.
A program may use at most 128 MiB of HBM per device.

```python
import jax
import jax.numpy as jnp
from jax import lax

ROW_CHANNEL_SIZE = 64
HIDDEN_WIDTH = 32
C_Z = 128
R_DEV = 8
RELATED_SEQS = 512
PROTEIN_SPAN = 128


def shard_levels(rng, dims, shards, least, top_value):
    def one(axis_at, blocks):
        heights = jax.random.uniform(jax.random.fold_in(jax.random.fold_in(rng, 6), axis_at), (blocks,), jnp.float32, least / len(shards), top_value / len(shards))
        return jnp.repeat(jnp.exp(heights), dims[axis_at] // blocks).reshape((-1,) + (1,) * (len(dims) - axis_at - 1))

    level = one(*shards[0])
    for cut in shards[1:]:
        level = level * one(*cut)
    return level


def centred(own_key, extent, width, most, shards=(), dtype=jnp.bfloat16):
    level = shard_levels(own_key, extent, shards, -0.22, 0.18) if shards else 1.0
    values = jax.random.normal(own_key, extent, jnp.float32) * width * level
    return jnp.minimum(jnp.maximum(values, -most), most).astype(dtype)


def setup_inputs(seed: int = 0, part: int = 0) -> dict:
    arg_keys = jax.random.split(jax.random.key(seed), 8)
    part_keys = jax.random.split(jax.random.fold_in(arg_keys[7], part), 8)
    stacked_sequence_embedding = centred(part_keys[0], (RELATED_SEQS, PROTEIN_SPAN * ROW_CHANNEL_SIZE), 1.0, 6.0, ((0, 16),))
    normalizer_multiplier = jnp.clip(1.0 + 0.18 * jax.random.normal(arg_keys[1], (ROW_CHANNEL_SIZE,), jnp.float32), 0.1, 1.9)
    normalizer_additive = centred(arg_keys[2], (ROW_CHANNEL_SIZE,), 0.4, 2.0, (), jnp.float32)
    lhs_projected_tensor = centred(arg_keys[3], (ROW_CHANNEL_SIZE, HIDDEN_WIDTH), ROW_CHANNEL_SIZE ** -0.5, 0.75)
    rhs_projected_tensor = centred(arg_keys[4], (ROW_CHANNEL_SIZE, HIDDEN_WIDTH), ROW_CHANNEL_SIZE ** -0.5, 0.75)
    pairwise_matrix = centred(arg_keys[5], (HIDDEN_WIDTH * HIDDEN_WIDTH, C_Z), 0.06, 0.359375)
    pairwise_shift = centred(arg_keys[6], (C_Z,), 0.5, 3.0, (), jnp.float32)
    return {"stacked_sequence_embedding": stacked_sequence_embedding, "normalizer_multiplier": normalizer_multiplier, "normalizer_additive": normalizer_additive, "lhs_projected_tensor": lhs_projected_tensor, "rhs_projected_tensor": rhs_projected_tensor, "pairwise_matrix": pairwise_matrix, "pairwise_shift": pairwise_shift}


def normalize(member_list, normalizer_multiplier, normalizer_additive):
    center = member_list - lax.optimization_barrier(jnp.mean(member_list, axis=-1, keepdims=True))
    spread = lax.optimization_barrier(jnp.mean(center * center, axis=-1, keepdims=True))
    return (center * lax.rsqrt(spread + 1e-05) * normalizer_multiplier + normalizer_additive).astype(jnp.bfloat16)

def reference(stacked_sequence_embedding, normalizer_multiplier, normalizer_additive, lhs_projected_tensor, rhs_projected_tensor, pairwise_matrix, pairwise_shift):
    member_list = stacked_sequence_embedding.astype(jnp.float32).reshape(RELATED_SEQS * PROTEIN_SPAN, ROW_CHANNEL_SIZE)
    normed = normalize(member_list, normalizer_multiplier, normalizer_additive)
    left = jnp.dot(normed, lhs_projected_tensor, preferred_element_type=jnp.float32).astype(jnp.bfloat16).reshape(RELATED_SEQS, PROTEIN_SPAN * HIDDEN_WIDTH)
    right = jnp.dot(normed, rhs_projected_tensor, preferred_element_type=jnp.float32).astype(jnp.bfloat16).reshape(RELATED_SEQS, PROTEIN_SPAN * HIDDEN_WIDTH)
    left_blocks = left.reshape(RELATED_SEQS, PROTEIN_SPAN // R_DEV, R_DEV * HIDDEN_WIDTH).transpose(1, 0, 2)

    def one_block(block):
        outer = lax.dot_general(block.astype(jnp.float32), right.astype(jnp.float32), (((0,), (0,)), ((), ()))) / RELATED_SEQS
        flat = outer.reshape(R_DEV, HIDDEN_WIDTH, PROTEIN_SPAN, HIDDEN_WIDTH).transpose(0, 2, 1, 3).reshape(R_DEV * PROTEIN_SPAN, HIDDEN_WIDTH * HIDDEN_WIDTH).astype(jnp.bfloat16)
        mapped = jnp.dot(flat, pairwise_matrix, preferred_element_type=jnp.float32) + pairwise_shift
        return mapped.astype(jnp.bfloat16).reshape(R_DEV, PROTEIN_SPAN, C_Z)
    tiles = lax.map(one_block, left_blocks)
    return tiles.reshape(PROTEIN_SPAN, PROTEIN_SPAN, C_Z)
```

```python
import functools

import jax
import jax.numpy as jnp
from jax import lax
from jax.experimental import pallas as pl
from jax.experimental.pallas import tpu as pltpu
from jax.sharding import PartitionSpec as P

F32 = jnp.float32
BF16 = jnp.bfloat16
LANES = 128
PARTS = 4


def dot(a, b):
    return jnp.dot(a, b, preferred_element_type=F32)


def kernel(
    n,
    x_ref,
    gain_ref,
    offset_ref,
    lhs_ref,
    rhs_ref,
    pair_ref,
    shift_ref,
    out_ref,
    norm_scr,
    turn_scr,
    pair_scr,
    pair_t,
    left_send,
    left_all,
    left_t,
    right_all,
    flat,
    mix,
    l_send,
    l_recv,
    ring_send,
    ring_recv,
    peer_send,
    peer_recv,
):
    rows = x_ref.shape[0]
    chans, width = lhs_ref.shape
    residues = x_ref.shape[1] // chans
    resid = residues // n
    tiles = x_ref.shape[1] // LANES
    per_tile = LANES // chans
    chips = n // 2
    me = lax.axis_index("res")
    core = lax.rem(me, 2)
    chip = me // 2

    col = lax.rem(chip, 2)
    place = (chip // 2) * (1 - 2 * col) + col * (chips - 1)

    def device_at(where):
        where = lax.rem(where + chips, chips)
        back = where // (chips // 2)
        return 2 * ((1 - back) * (2 * where) + back * (2 * (chips - 1 - where) + 1)) + core

    peer = me + 1 - 2 * core
    right_dev = device_at(place + 1)
    left_dev = device_at(place - 1)

    barrier = pltpu.get_barrier_semaphore()

    def greet(k, carry):
        pl.semaphore_signal(
            barrier,
            inc=1,
            device_id={"res": lax.rem(me + k, n)},
            device_id_type=pl.DeviceIdType.MESH,
        )
        return carry

    lax.fori_loop(1, n, greet, 0)

    def same(shape, down, across):
        r = lax.broadcasted_iota(jnp.int32, shape, 0) // down
        c = lax.broadcasted_iota(jnp.int32, shape, 1) // across
        return r == c

    lhs = lhs_ref[...].astype(F32)
    reps = LANES // width
    lhs_wide = jnp.concatenate([lhs] * reps, axis=1)
    lhs_wide = jnp.concatenate([lhs_wide] * reps, axis=0)
    lhs_wide = jnp.where(same(lhs_wide.shape, chans, width), lhs_wide, 0.0).astype(BF16)
    rhs = rhs_ref[...].astype(F32)
    rhs_wide = jnp.concatenate([rhs] * reps, axis=1)
    rhs_wide = jnp.concatenate([rhs_wide] * per_tile, axis=0)
    rhs_t = rhs_wide.T[:width, :].astype(BF16)
    averager = jnp.where(same((LANES, LANES), chans, chans), 1.0 / chans, 0.0).astype(BF16)
    gain = jnp.concatenate([gain_ref[...]] * per_tile, axis=1)
    offset = jnp.concatenate([offset_ref[...]] * per_tile, axis=1)

    group = 8
    dests = group * per_tile // resid
    halves = resid * width // LANES

    def project(b, carry):
        x = jnp.concatenate(
            [
                x_ref[:, pl.ds(pl.multiple_of((b * group + u) * LANES, LANES), LANES)].astype(F32)
                for u in range(group)
            ],
            axis=0,
        )
        center = x - dot(x.astype(BF16), averager)
        square = center * center
        high = square.astype(BF16)
        low = (square - high.astype(F32)).astype(BF16)
        spread = dot(high, averager) + dot(low, averager)
        normed = (center * lax.rsqrt(spread + 1e-05) * gain + offset).astype(BF16)
        wide = normed.astype(F32)
        norm_scr[pl.ds(pl.multiple_of(b * group * rows, 8), group * rows), :] = wide
        even = jnp.concatenate(
            [wide[u * rows : (u + 1) * rows] for u in range(0, group, 2)], axis=0
        ).astype(BF16)
        odd = jnp.concatenate(
            [wide[u * rows : (u + 1) * rows] for u in range(1, group, 2)], axis=0
        ).astype(BF16)
        left = dot(jnp.concatenate([even, odd], axis=1), lhs_wide)
        for u in range(group // 2):
            left_send[b * dests + u // halves, :, (u % halves) * LANES : (u % halves + 1) * LANES] = (
                left[u * rows : (u + 1) * rows].astype(BF16)
            )
        return carry

    lax.fori_loop(0, tiles // group, project, 0)

    lane = lax.broadcasted_iota(jnp.int32, (tiles, LANES), 1) // chans

    def turn(s, carry):
        one = norm_scr[pl.ds(s, tiles, stride=rows), :]
        spread_out = jnp.concatenate(
            [jnp.where(lane == r, one, 0.0) for r in range(per_tile)], axis=0
        ).astype(BF16)
        res = lax.dot_general(
            rhs_t, spread_out, (((1,), (1,)), ((), ())), preferred_element_type=F32
        )
        for j in range(residues // LANES):
            turn_scr[j, pl.ds(s, width, stride=rows), :] = res[:, j * LANES : (j + 1) * LANES]
        return carry

    lax.fori_loop(0, rows, turn, 0)
    for q in range(width):
        for j in range(residues // LANES):
            right_all[me, :, q * residues + j * LANES : q * residues + (j + 1) * LANES] = (
                turn_scr[j, q * rows : (q + 1) * rows, :].astype(BF16)
            )

    pl.semaphore_wait(barrier, n - 1)

    part = width * residues // PARTS

    def block(dev, h):
        return right_all.at[dev, :, pl.ds(h * part, part)]

    def ring(h, step, shift):
        sign = 1 - 2 * (h % 2)
        ref = block(device_at(place - sign * (step + shift)), h)
        return pltpu.make_async_remote_copy(
            src_ref=ref,
            dst_ref=ref,
            send_sem=ring_send.at[h, step],
            recv_sem=ring_recv.at[h, step],
            device_id={"res": right_dev if h % 2 == 0 else left_dev},
            device_id_type=pl.DeviceIdType.MESH,
        )

    def share(h, step, theirs):
        sign = 1 - 2 * (h % 2)
        source = device_at(place - sign * step)
        if theirs:
            source = source + 1 - 2 * core
        ref = block(source, h)
        return pltpu.make_async_remote_copy(
            src_ref=ref,
            dst_ref=ref,
            send_sem=peer_send.at[h, step],
            recv_sem=peer_recv.at[h, step],
            device_id={"res": peer},
            device_id_type=pl.DeviceIdType.MESH,
        )

    def left_copy(k):
        to = lax.rem(me + k, n)
        return pltpu.make_async_remote_copy(
            src_ref=left_send.at[to],
            dst_ref=left_all.at[me],
            send_sem=l_send.at[k],
            recv_sem=l_recv.at[k],
            device_id={"res": to},
            device_id_type=pl.DeviceIdType.MESH,
        )

    for h in range(PARTS):
        ring(h, 0, 0).start()
    for h in range(PARTS):
        share(h, 0, False).start()

    def send_left(k, carry):
        left_copy(k).start()
        return carry

    lax.fori_loop(1, n, send_left, 0)
    left_all[me] = left_send[me]

    pair_scr[...] = pair_ref[...].astype(F32)
    for b in range(width // reps):
        some = jnp.concatenate(
            [pair_scr[pl.ds(b * reps + u, width, stride=width), :] for u in range(reps)], axis=0
        )
        pair_t[:, b * LANES : (b + 1) * LANES] = some.T.astype(BF16)

    def hop(step, carry):
        for h in range(PARTS):
            ring(h, step - 1, 1).wait_recv()
            ring(h, step, 0).start()
            share(h, step, False).start()
        return carry

    lax.fori_loop(1, chips - 1, hop, 0)
    for h in range(PARTS):
        ring(h, chips - 2, 1).wait_recv()
        share(h, chips - 1, False).start()

    def left_in(k, carry):
        source = lax.rem(me - k + n, n)
        pltpu.make_async_remote_copy(
            src_ref=left_send.at[source],
            dst_ref=left_all.at[source],
            send_sem=l_send.at[k],
            recv_sem=l_recv.at[k],
            device_id={"res": source},
            device_id_type=pl.DeviceIdType.MESH,
        ).wait_recv()
        return carry

    lax.fori_loop(1, n, left_in, 0)
    left_t[...] = (
        left_all[...].astype(F32).reshape(n * rows, resid * width).T.astype(BF16)
    )

    def peer_in(step, carry):
        for h in range(PARTS):
            share(h, step, True).wait_recv()
        return carry

    lax.fori_loop(0, chips, peer_in, 0)

    qs = 4
    total = n * rows

    def outer(b, carry):
        here = right_all[:, :, pl.ds(pl.multiple_of(b * qs * residues, LANES), qs * residues)]
        if rows % 16:
            here = here.astype(F32)
        here = here.reshape(total, qs * residues).astype(BF16)
        product = (dot(left_t[...], here) * (1.0 / total)).astype(BF16)
        for u in range(qs):
            for i in range(resid):
                flat[
                    pl.ds(pl.multiple_of((b * qs + u) * width, width), width),
                    i * residues : (i + 1) * residues,
                ] = product[i * width : (i + 1) * width, u * residues : (u + 1) * residues]
        return carry

    lax.fori_loop(0, width // qs, outer, 0)

    for i in range(0, resid, 2):
        mapped = dot(pair_t[...], flat[:, i * residues : (i + 2) * residues])
        for u in range(2):
            turned = mapped[:, u * residues : (u + 1) * residues].T + shift_ref[...]
            for r in range(per_tile):
                mix[i + u, pl.ds(r, tiles, stride=per_tile), :] = turned[
                    r * tiles : (r + 1) * tiles
                ]
            out_ref[i + u] = mix[i + u].astype(BF16)

    def drain(step, carry):
        for h in range(PARTS):
            ring(h, step, 0).wait_send()
            share(h, step, False).wait_send()
        return carry

    lax.fori_loop(0, chips - 1, drain, 0)
    for h in range(PARTS):
        share(h, chips - 1, False).wait_send()

    def left_out(k, carry):
        left_copy(k).wait_send()
        return carry

    lax.fori_loop(1, n, left_out, 0)


def on_device(n, x, gain, offset, lhs, rhs, pair, shift):
    rows = x.shape[0]
    chans, width = lhs.shape
    residues = x.shape[1] // chans
    resid = residues // n
    tiles = x.shape[1] // LANES
    chips = n // 2
    depth = width * width
    out_chans = pair.shape[1]
    vmem = pl.BlockSpec(memory_space=pltpu.VMEM)
    return pl.pallas_call(
        functools.partial(kernel, n),
        out_shape=jax.ShapeDtypeStruct((resid, residues, out_chans), BF16),
        in_specs=[vmem] * 7,
        out_specs=vmem,
        scratch_shapes=[
            pltpu.VMEM((tiles * rows, LANES), F32),
            pltpu.VMEM((residues // LANES, width * rows, LANES), F32),
            pltpu.VMEM((depth, out_chans), F32),
            pltpu.VMEM((out_chans, depth), BF16),
            pltpu.VMEM((n, rows, resid * width), BF16),
            pltpu.VMEM((n, rows, resid * width), BF16),
            pltpu.VMEM((resid * width, n * rows), BF16),
            pltpu.VMEM((n, rows, width * residues), BF16),
            pltpu.VMEM((depth, resid * residues), BF16),
            pltpu.VMEM((resid, residues, out_chans), F32),
            pltpu.SemaphoreType.DMA((n,)),
            pltpu.SemaphoreType.DMA((n,)),
            pltpu.SemaphoreType.DMA((PARTS, chips)),
            pltpu.SemaphoreType.DMA((PARTS, chips)),
            pltpu.SemaphoreType.DMA((PARTS, chips)),
            pltpu.SemaphoreType.DMA((PARTS, chips)),
        ],
        compiler_params=pltpu.CompilerParams(
            collective_id=0, has_side_effects=True, vmem_limit_bytes=56 * 1024 * 1024
        ),
    )(x, gain.reshape(1, -1), offset.reshape(1, -1), lhs, rhs, pair, shift.reshape(1, -1))


def solution(mesh):
    in_specs = (P(("grp", "res"), None), P(), P(), P(), P(), P(), P())
    out_specs = P(("grp", "res"), None, None)
    return jax.shard_map(
        functools.partial(on_device, mesh.shape["res"]),
        mesh=mesh,
        in_specs=in_specs,
        out_specs=out_specs,
        check_vma=False,
    )
```

```python
import functools

import jax
import jax.numpy as jnp
from jax import lax
from jax.experimental import pallas as pl
from jax.experimental.pallas import tpu as pltpu
from jax.sharding import PartitionSpec as P

F32 = jnp.float32
BF16 = jnp.bfloat16
LANES = 128
PARTS = 2


def dot(a, b):
    return jnp.dot(a, b, preferred_element_type=F32)


def kernel(
    n,
    x_ref,
    gain_ref,
    offset_ref,
    lhs_ref,
    rhs_ref,
    pair_ref,
    shift_ref,
    out_ref,
    norm_scr,
    turn_scr,
    pair_scr,
    pair_t,
    left_send,
    left_all,
    left_t,
    right_all,
    flat,
    mix,
    sum_send,
    sum_recv,
    l_send,
    l_recv,
    r_send,
    r_recv,
    peer_send,
    peer_recv,
    s_send,
    s_recv,
):
    rows = x_ref.shape[0]
    width, chans = lhs_ref.shape
    residues = x_ref.shape[1] // chans
    resid = residues // n
    tiles = x_ref.shape[1] // LANES
    per_tile = LANES // chans
    team = n // 2
    chips = team // 2
    me = lax.axis_index("res")
    half = me // team
    seat = lax.rem(me, team)
    core = lax.rem(seat, 2)
    chip = seat // 2
    base = half * team
    partner = (1 - half) * team + seat
    peer_seat = seat + 1 - 2 * core

    def to(dev):
        return dict(device_id={"res": dev}, device_id_type=pl.DeviceIdType.MESH)

    barrier = pltpu.get_barrier_semaphore()

    def greet(k, carry):
        pl.semaphore_signal(barrier, inc=1, **to(base + lax.rem(seat + k, team)))
        return carry

    lax.fori_loop(1, team, greet, 0)
    pl.semaphore_signal(barrier, inc=1, **to(partner))

    def same(shape, down, across):
        r = lax.broadcasted_iota(jnp.int32, shape, 0) // down
        c = lax.broadcasted_iota(jnp.int32, shape, 1) // across
        return r == c

    reps = LANES // width
    lhs = jnp.concatenate([lhs_ref[...].astype(F32)] * per_tile, axis=1)
    lhs = jnp.concatenate([lhs] * reps, axis=0).T
    lhs_wide = jnp.concatenate([lhs] * (reps // per_tile), axis=0)
    lhs_wide = jnp.where(same(lhs_wide.shape, chans, width), lhs_wide, 0.0).astype(BF16)
    rhs_t = jnp.concatenate([rhs_ref[...].astype(F32)] * per_tile, axis=1).astype(BF16)
    averager = jnp.where(same((LANES, LANES), chans, chans), 1.0 / chans, 0.0).astype(BF16)
    gain = jnp.concatenate([gain_ref[...]] * per_tile, axis=1)
    offset = jnp.concatenate([offset_ref[...]] * per_tile, axis=1)

    group = 8
    dests = group * per_tile // resid
    halves = resid * width // LANES

    def project(b, carry):
        x = jnp.concatenate(
            [
                x_ref[:, pl.ds(pl.multiple_of((b * group + u) * LANES, LANES), LANES)].astype(F32)
                for u in range(group)
            ],
            axis=0,
        )
        center = x - dot(x.astype(BF16), averager)
        square = center * center
        high = square.astype(BF16)
        low = (square - high.astype(F32)).astype(BF16)
        spread = dot(high, averager) + dot(low, averager)
        normed = (center * lax.rsqrt(spread + 1e-05) * gain + offset).astype(BF16)
        wide = normed.astype(F32)
        norm_scr[pl.ds(pl.multiple_of(b * group * rows, 8), group * rows), :] = wide
        even = jnp.concatenate(
            [wide[u * rows : (u + 1) * rows] for u in range(0, group, 2)], axis=0
        ).astype(BF16)
        odd = jnp.concatenate(
            [wide[u * rows : (u + 1) * rows] for u in range(1, group, 2)], axis=0
        ).astype(BF16)
        left = dot(jnp.concatenate([even, odd], axis=1), lhs_wide)
        for u in range(group // 2):
            dest = b * dests + u // halves
            left_send[
                lax.rem(dest, team), dest // team, :, (u % halves) * LANES : (u % halves + 1) * LANES
            ] = left[u * rows : (u + 1) * rows].astype(BF16)
        return carry

    lax.fori_loop(0, tiles // group, project, 0)

    lane = lax.broadcasted_iota(jnp.int32, (tiles, LANES), 1) // chans

    def turn(s, carry):
        one = norm_scr[pl.ds(s, tiles, stride=rows), :]
        spread_out = jnp.concatenate(
            [jnp.where(lane == r, one, 0.0) for r in range(per_tile)], axis=0
        ).astype(BF16)
        res = lax.dot_general(
            rhs_t, spread_out, (((1,), (1,)), ((), ())), preferred_element_type=F32
        )
        for j in range(residues // LANES):
            turn_scr[j, pl.ds(s, width, stride=rows), :] = res[:, j * LANES : (j + 1) * LANES]
        return carry

    lax.fori_loop(0, rows, turn, 0)
    for q in range(width):
        for j in range(residues // LANES):
            right_all[seat, :, q * residues + j * LANES : q * residues + (j + 1) * LANES] = (
                turn_scr[j, q * rows : (q + 1) * rows, :].astype(BF16)
            )

    pl.semaphore_wait(barrier, team)

    part = width * residues // PARTS

    def block(at, h):
        return right_all.at[at, :, pl.ds(h * part, part)]

    def right_copy(k, h, incoming):
        other = 2 * lax.rem(chip + k + chips, chips) + core
        ref = block(other if incoming else seat, h)
        slot = chips - k if incoming else k
        return pltpu.make_async_remote_copy(
            src_ref=ref,
            dst_ref=ref,
            send_sem=r_send.at[h, slot],
            recv_sem=r_recv.at[h, slot],
            **to(base + other),
        )

    def share(k, h, theirs):
        source = 2 * lax.rem(chip + k, chips) + (1 - core if theirs else core)
        ref = block(source, h)
        return pltpu.make_async_remote_copy(
            src_ref=ref,
            dst_ref=ref,
            send_sem=peer_send.at[h, k],
            recv_sem=peer_recv.at[h, k],
            **to(base + peer_seat),
        )

    def left_copy(k, incoming):
        slot = team - k if incoming else k
        other = lax.rem(seat + k, team)
        return pltpu.make_async_remote_copy(
            src_ref=left_send.at[other],
            dst_ref=left_all.at[other if incoming else seat],
            send_sem=l_send.at[slot],
            recv_sem=l_recv.at[slot],
            **to(base + other),
        )

    def over(first, last, act):
        def step(k, carry):
            act(k)
            return carry

        lax.fori_loop(first, last, step, 0)

    for h in range(PARTS):
        over(1, chips, lambda k: right_copy(k, h, False).start())
        share(0, h, False).start()
    over(1, team, lambda k: left_copy(k, False).start())
    left_all[seat] = left_send[seat]

    pair_scr[...] = pair_ref[...].astype(F32)
    for b in range(width // reps):
        some = jnp.concatenate(
            [pair_scr[pl.ds(b * reps + u, width, stride=width), :] for u in range(reps)], axis=0
        )
        pair_t[:, b * LANES : (b + 1) * LANES] = some.T.astype(BF16)

    for h in range(PARTS):

        def pass_on(k):
            right_copy(k, h, True).wait_recv()
            share(k, h, False).start()

        over(1, chips, pass_on)
    over(1, team, lambda k: left_copy(k, True).wait_recv())
    for b in range(2):
        left_t[b] = (
            left_all[:, b].astype(F32).reshape(team * rows, resid * width).T.astype(BF16)
        )
    for h in range(PARTS):
        over(0, chips, lambda k: share(k, h, True).wait_recv())

    qs = 4
    here_rows = team * rows
    total = n * rows

    def fill(which):
        def outer(b):
            here = right_all[:, :, pl.ds(pl.multiple_of(b * qs * residues, LANES), qs * residues)]
            if rows % 16:
                here = here.astype(F32)
            here = here.reshape(here_rows, qs * residues).astype(BF16)
            product = (dot(left_t[which], here) * (1.0 / total)).astype(BF16)
            for u in range(qs):
                for i in range(resid):
                    flat[
                        pl.ds(pl.multiple_of((b * qs + u) * width, width), width),
                        i * residues : (i + 1) * residues,
                    ] = product[i * width : (i + 1) * width, u * residues : (u + 1) * residues]

        over(0, width // qs, outer)

    def sums(b):
        return pltpu.make_async_remote_copy(
            src_ref=sum_send.at[b],
            dst_ref=sum_recv.at[b],
            send_sem=s_send.at[b],
            recv_sem=s_recv.at[b],
            **to(partner),
        )

    def mapped(b):
        return dot(pair_t[...], flat[:, b * 2 * residues : (b + 1) * 2 * residues])

    fill(1 - half)
    for b in range(resid // 2):
        sum_send[b] = mapped(b).astype(BF16)
        sums(b).start()
    fill(half)
    for b in range(resid // 2):
        mine = mapped(b)
        sums(b).wait_recv()
        mine = mine + sum_recv[b].astype(F32)
        for u in range(2):
            turned = mine[:, u * residues : (u + 1) * residues].T + shift_ref[...]
            for r in range(per_tile):
                mix[2 * b + u, pl.ds(r, tiles, stride=per_tile), :] = turned[
                    r * tiles : (r + 1) * tiles
                ]
            out_ref[2 * b + u] = mix[2 * b + u].astype(BF16)

    for h in range(PARTS):
        over(1, chips, lambda k: right_copy(k, h, False).wait_send())
        over(0, chips, lambda k: share(k, h, False).wait_send())
    over(1, team, lambda k: left_copy(k, False).wait_send())
    for b in range(resid // 2):
        sums(b).wait_send()


def on_device(n, x, gain, offset, lhs, rhs, pair, shift):
    rows = x.shape[0]
    chans, width = lhs.shape
    residues = x.shape[1] // chans
    resid = residues // n
    tiles = x.shape[1] // LANES
    team = n // 2
    chips = team // 2
    depth = width * width
    out_chans = pair.shape[1]
    vmem = pl.BlockSpec(memory_space=pltpu.VMEM)
    return pl.pallas_call(
        functools.partial(kernel, n),
        out_shape=jax.ShapeDtypeStruct((resid, residues, out_chans), BF16),
        in_specs=[vmem] * 7,
        out_specs=vmem,
        scratch_shapes=[
            pltpu.VMEM((tiles * rows, LANES), F32),
            pltpu.VMEM((residues // LANES, width * rows, LANES), F32),
            pltpu.VMEM((depth, out_chans), F32),
            pltpu.VMEM((out_chans, depth), BF16),
            pltpu.VMEM((team, 2, rows, resid * width), BF16),
            pltpu.VMEM((team, 2, rows, resid * width), BF16),
            pltpu.VMEM((2, resid * width, team * rows), BF16),
            pltpu.VMEM((team, rows, width * residues), BF16),
            pltpu.VMEM((depth, resid * residues), BF16),
            pltpu.VMEM((resid, residues, out_chans), F32),
            pltpu.VMEM((resid // 2, out_chans, 2 * residues), BF16),
            pltpu.VMEM((resid // 2, out_chans, 2 * residues), BF16),
            pltpu.SemaphoreType.DMA((team,)),
            pltpu.SemaphoreType.DMA((team,)),
            pltpu.SemaphoreType.DMA((PARTS, chips)),
            pltpu.SemaphoreType.DMA((PARTS, chips)),
            pltpu.SemaphoreType.DMA((PARTS, chips)),
            pltpu.SemaphoreType.DMA((PARTS, chips)),
            pltpu.SemaphoreType.DMA((resid // 2,)),
            pltpu.SemaphoreType.DMA((resid // 2,)),
        ],
        compiler_params=pltpu.CompilerParams(
            collective_id=0, has_side_effects=True, vmem_limit_bytes=56 * 1024 * 1024
        ),
    )(x, gain.reshape(1, -1), offset.reshape(1, -1), lhs.T, rhs.T, pair, shift.reshape(1, -1))


def solution(mesh):
    in_specs = (P(("grp", "res"), None), P(), P(), P(), P(), P(), P())
    out_specs = P(("grp", "res"), None, None)
    return jax.shard_map(
        functools.partial(on_device, mesh.shape["res"]),
        mesh=mesh,
        in_specs=in_specs,
        out_specs=out_specs,
        check_vma=False,
    )
```

```python
import functools

import jax
import jax.numpy as jnp
from jax import lax
from jax.experimental import pallas as pl
from jax.experimental.pallas import tpu as pltpu
from jax.sharding import PartitionSpec as P

F32 = jnp.float32
BF16 = jnp.bfloat16
LANES = 128
WAVES = 2


def dot(a, b):
    return jnp.dot(a, b, preferred_element_type=F32)


def kernel(
    n,
    x_ref,
    gain_ref,
    offset_ref,
    lhs_ref,
    rhs_ref,
    pair_ref,
    shift_ref,
    out_ref,
    norm_scr,
    turn_scr,
    pair_scr,
    pair_t,
    left_send,
    left_all,
    left_t,
    right_all,
    flat,
    mix,
    kept,
    sum_send,
    sum_recv,
    l_send,
    l_recv,
    r_send,
    r_recv,
    peer_send,
    peer_recv,
    s_send,
    s_recv,
):
    rows = x_ref.shape[0]
    width, chans = lhs_ref.shape
    residues = x_ref.shape[1] // chans
    resid = residues // n
    tiles = x_ref.shape[1] // LANES
    per_tile = LANES // chans
    team = n // 2
    chips = team // 2
    me = lax.axis_index("res")
    half = me // team
    seat = lax.rem(me, team)
    core = lax.rem(seat, 2)
    chip = seat // 2
    base = half * team
    partner = (1 - half) * team + seat
    peer_seat = seat + 1 - 2 * core

    def to(dev):
        return dict(device_id={"res": dev}, device_id_type=pl.DeviceIdType.MESH)

    barrier = pltpu.get_barrier_semaphore()

    def greet(k, carry):
        pl.semaphore_signal(barrier, inc=1, **to(base + lax.rem(seat + k, team)))
        return carry

    lax.fori_loop(1, team, greet, 0)
    pl.semaphore_signal(barrier, inc=1, **to(partner))

    def same(shape, down, across):
        r = lax.broadcasted_iota(jnp.int32, shape, 0) // down
        c = lax.broadcasted_iota(jnp.int32, shape, 1) // across
        return r == c

    reps = LANES // width
    lhs = jnp.concatenate([lhs_ref[...].astype(F32)] * per_tile, axis=1)
    lhs = jnp.concatenate([lhs] * reps, axis=0).T
    lhs_wide = jnp.concatenate([lhs] * (reps // per_tile), axis=0)
    lhs_wide = jnp.where(same(lhs_wide.shape, chans, width), lhs_wide, 0.0).astype(BF16)
    fold = width // 2
    rhs = rhs_ref[...].astype(F32)
    rhs_t = jnp.concatenate([rhs[:fold], rhs[fold:]], axis=1).astype(BF16)
    averager = jnp.where(same((LANES, LANES), chans, chans), 1.0 / chans, 0.0).astype(BF16)
    gain = jnp.concatenate([gain_ref[...]] * per_tile, axis=1)
    offset = jnp.concatenate([offset_ref[...]] * per_tile, axis=1)

    group = 8
    dests = group * per_tile // resid
    halves = resid * width // LANES

    def project(b, carry):
        x = jnp.concatenate(
            [
                x_ref[:, pl.ds(pl.multiple_of((b * group + u) * LANES, LANES), LANES)].astype(F32)
                for u in range(group)
            ],
            axis=0,
        )
        center = x - dot(x.astype(BF16), averager)
        square = center * center
        high = square.astype(BF16)
        low = (square - high.astype(F32)).astype(BF16)
        spread = dot(high, averager) + dot(low, averager)
        normed = (center * lax.rsqrt(spread + 1e-05) * gain + offset).astype(BF16)
        wide = normed.astype(F32)
        norm_scr[pl.ds(pl.multiple_of(b * group * rows, 8), group * rows), :] = wide
        even = jnp.concatenate(
            [wide[u * rows : (u + 1) * rows] for u in range(0, group, 2)], axis=0
        ).astype(BF16)
        odd = jnp.concatenate(
            [wide[u * rows : (u + 1) * rows] for u in range(1, group, 2)], axis=0
        ).astype(BF16)
        left = dot(jnp.concatenate([even, odd], axis=1), lhs_wide)
        for u in range(group // 2):
            dest = b * dests + u // halves
            left_send[
                lax.rem(dest, team), dest // team, :, (u % halves) * LANES : (u % halves + 1) * LANES
            ] = left[u * rows : (u + 1) * rows].astype(BF16)
        return carry

    lax.fori_loop(0, tiles // group, project, 0)

    pl.semaphore_wait(barrier, team)

    part = width * residues // WAVES

    def block(at, h):
        return right_all.at[at, :, pl.ds(h * part, part)]

    def right_copy(k, h, incoming):
        other = 2 * lax.rem(chip + k + chips, chips) + core
        ref = block(other if incoming else seat, h)
        slot = chips - k if incoming else k
        return pltpu.make_async_remote_copy(
            src_ref=ref,
            dst_ref=ref,
            send_sem=r_send.at[h, slot],
            recv_sem=r_recv.at[h, slot],
            **to(base + other),
        )

    def share(k, h, theirs):
        source = 2 * lax.rem(chip + k, chips) + (1 - core if theirs else core)
        ref = block(source, h)
        return pltpu.make_async_remote_copy(
            src_ref=ref,
            dst_ref=ref,
            send_sem=peer_send.at[h, k],
            recv_sem=peer_recv.at[h, k],
            **to(base + peer_seat),
        )

    def left_copy(k, incoming):
        slot = team - k if incoming else k
        other = lax.rem(seat + k, team)
        return pltpu.make_async_remote_copy(
            src_ref=left_send.at[other],
            dst_ref=left_all.at[other if incoming else seat],
            send_sem=l_send.at[slot],
            recv_sem=l_recv.at[slot],
            **to(base + other),
        )

    def over(first, last, act):
        def step(k, carry):
            act(k)
            return carry

        lax.fori_loop(first, last, step, 0)

    over(1, team, lambda k: left_copy(k, False).start())

    lane = lax.broadcasted_iota(jnp.int32, (tiles, LANES), 1) // chans
    strips = residues // LANES

    def turn(s):
        one = norm_scr[pl.ds(s, tiles, stride=rows), :]
        swapped = pltpu.roll(one, chans, 1)
        spread_out = jnp.concatenate(
            [
                jnp.where(lane == q, one if q == r else swapped, 0.0)
                for r in range(2)
                for q in range(2)
            ],
            axis=0,
        ).astype(BF16)
        res = lax.dot_general(
            rhs_t, spread_out, (((1,), (1,)), ((), ())), preferred_element_type=F32
        )
        for j in range(2 * strips):
            turn_scr[j, pl.ds(s, fold, stride=rows), :] = res[:, j * LANES : (j + 1) * LANES]

    over(0, rows, turn)
    for h in range(WAVES):
        for q in range(fold):
            for j in range(strips):
                at = (h * fold + q) * residues + j * LANES
                right_all[seat, :, at : at + LANES] = turn_scr[
                    h * strips + j, q * rows : (q + 1) * rows, :
                ].astype(BF16)
        over(1, chips, lambda k: right_copy(k, h, False).start())
        share(0, h, False).start()
    left_all[seat] = left_send[seat]

    out_chans = pair_ref.shape[1]
    pair_scr[...] = pair_ref[...].astype(F32)
    for c in range(2):
        for b in range(fold // reps):
            some = jnp.concatenate(
                [
                    pair_scr[pl.ds(c * fold + b * reps + u, width, stride=width), :]
                    for u in range(reps)
                ],
                axis=0,
            )
            pair_t[c * out_chans : (c + 1) * out_chans, b * LANES : (b + 1) * LANES] = (
                some.T.astype(BF16)
            )

    def gather(h):
        def pass_on(k):
            right_copy(k, h, True).wait_recv()
            share(k, h, False).start()

        over(1, chips, pass_on)

    def gathered(h):
        over(0, chips, lambda k: share(k, h, True).wait_recv())

    qs = 4
    here_rows = team * rows
    total = n * rows
    first = lax.broadcasted_iota(jnp.int32, (out_chans, residues), 1) < tiles

    def fill(which, h):
        def outer(b):
            here = right_all[
                :,
                :,
                pl.ds(
                    pl.multiple_of(h * fold * residues + b * qs * residues, LANES), qs * residues
                ),
            ]
            if rows % 16:
                here = here.astype(F32)
            here = here.reshape(here_rows, qs * residues).astype(BF16)
            product = (dot(left_t[which], here) * (1.0 / total)).astype(BF16)
            for u in range(qs):
                for i in range(resid):
                    flat[
                        pl.ds(pl.multiple_of((b * qs + u) * width, width), width),
                        i * residues : (i + 1) * residues,
                    ] = product[i * width : (i + 1) * width, u * residues : (u + 1) * residues]

        over(0, fold // qs, outer)

    def sums(b, h):
        return pltpu.make_async_remote_copy(
            src_ref=sum_send.at[h, b],
            dst_ref=sum_recv.at[h, b],
            send_sem=s_send.at[h, b],
            recv_sem=s_recv.at[h, b],
            **to(partner),
        )

    def mapped(b):
        both = dot(pair_t[...], flat[:, b * 2 * residues : (b + 1) * 2 * residues])
        low, high = both[:out_chans], both[out_chans:]
        one = low[:, :residues] + pltpu.roll(high[:, :residues], tiles, 1)
        two = pltpu.roll(low[:, residues:], tiles, 1) + high[:, residues:]
        return jnp.where(first, one, two)

    def theirs(h):
        fill(1 - half, h)
        for b in range(resid // 2):
            sum_send[h, b] = mapped(b).astype(BF16)
            sums(b, h).start()

    def mine(h):
        fill(half, h)
        for b in range(resid // 2):
            kept[h, b] = mapped(b)

    def finish(h):
        for b in range(resid // 2):
            sums(b, h).wait_recv()
            turned = (kept[h, b] + sum_recv[h, b].astype(F32)).T + shift_ref[...]
            for u in range(2):
                mix[2 * b + u, pl.ds(h, tiles, stride=2), :] = turned[u * tiles : (u + 1) * tiles]

    gather(0)
    over(1, team, lambda k: left_copy(k, True).wait_recv())
    for b in range(2):
        left_t[b] = (
            left_all[:, b].astype(F32).reshape(team * rows, resid * width).T.astype(BF16)
        )
    gathered(0)
    theirs(0)
    gather(1)
    mine(0)
    gathered(1)
    theirs(1)
    mine(1)
    finish(0)
    finish(1)
    for i in range(resid):
        out_ref[i] = mix[i].astype(BF16)

    for h in range(WAVES):
        over(1, chips, lambda k: right_copy(k, h, False).wait_send())
        over(0, chips, lambda k: share(k, h, False).wait_send())
    over(1, team, lambda k: left_copy(k, False).wait_send())
    for h in range(WAVES):
        for b in range(resid // 2):
            sums(b, h).wait_send()


def on_device(n, x, gain, offset, lhs, rhs, pair, shift):
    rows = x.shape[0]
    chans, width = lhs.shape
    residues = x.shape[1] // chans
    resid = residues // n
    tiles = x.shape[1] // LANES
    team = n // 2
    chips = team // 2
    depth = width * width
    out_chans = pair.shape[1]
    vmem = pl.BlockSpec(memory_space=pltpu.VMEM)
    return pl.pallas_call(
        functools.partial(kernel, n),
        out_shape=jax.ShapeDtypeStruct((resid, residues, out_chans), BF16),
        in_specs=[vmem] * 7,
        out_specs=vmem,
        scratch_shapes=[
            pltpu.VMEM((tiles * rows, LANES), F32),
            pltpu.VMEM((2 * residues // LANES, width // 2 * rows, LANES), F32),
            pltpu.VMEM((depth, out_chans), F32),
            pltpu.VMEM((2 * out_chans, depth // 2), BF16),
            pltpu.VMEM((team, 2, rows, resid * width), BF16),
            pltpu.VMEM((team, 2, rows, resid * width), BF16),
            pltpu.VMEM((2, resid * width, team * rows), BF16),
            pltpu.VMEM((team, rows, width * residues), BF16),
            pltpu.VMEM((depth // 2, resid * residues), BF16),
            pltpu.VMEM((resid, residues, out_chans), F32),
            pltpu.VMEM((WAVES, resid // 2, out_chans, residues), F32),
            pltpu.VMEM((WAVES, resid // 2, out_chans, residues), BF16),
            pltpu.VMEM((WAVES, resid // 2, out_chans, residues), BF16),
            pltpu.SemaphoreType.DMA((team,)),
            pltpu.SemaphoreType.DMA((team,)),
            pltpu.SemaphoreType.DMA((WAVES, chips)),
            pltpu.SemaphoreType.DMA((WAVES, chips)),
            pltpu.SemaphoreType.DMA((WAVES, chips)),
            pltpu.SemaphoreType.DMA((WAVES, chips)),
            pltpu.SemaphoreType.DMA((WAVES, resid // 2)),
            pltpu.SemaphoreType.DMA((WAVES, resid // 2)),
        ],
        compiler_params=pltpu.CompilerParams(
            collective_id=0, has_side_effects=True, vmem_limit_bytes=56 * 1024 * 1024
        ),
    )(x, gain.reshape(1, -1), offset.reshape(1, -1), lhs.T, rhs.T, pair, shift.reshape(1, -1))


def solution(mesh):
    in_specs = (P(("grp", "res"), None), P(), P(), P(), P(), P(), P())
    out_specs = P(("grp", "res"), None, None)
    return jax.shard_map(
        functools.partial(on_device, mesh.shape["res"]),
        mesh=mesh,
        in_specs=in_specs,
        out_specs=out_specs,
        check_vma=False,
    )
```

```python
import functools

import jax
import jax.numpy as jnp
from jax import lax
from jax.experimental import pallas as pl
from jax.experimental.pallas import tpu as pltpu
from jax.sharding import PartitionSpec as P

F32 = jnp.float32
BF16 = jnp.bfloat16
LANES = 128
WAVES = 2


def dot(a, b):
    return jnp.dot(a, b, preferred_element_type=F32)


def kernel(
    n,
    x_ref,
    gain_ref,
    offset_ref,
    lhs_ref,
    rhs_ref,
    pair_ref,
    shift_ref,
    out_ref,
    norm_scr,
    turn_scr,
    pair_scr,
    pair_t,
    left_send,
    left_all,
    left_t,
    right_all,
    flat,
    mix,
    kept,
    sum_send,
    sum_recv,
    l_send,
    l_recv,
    r_send,
    r_recv,
    peer_send,
    peer_recv,
    s_send,
    s_recv,
):
    rows = x_ref.shape[0]
    width, chans = lhs_ref.shape
    residues = x_ref.shape[1] // chans
    resid = residues // n
    tiles = x_ref.shape[1] // LANES
    per_tile = LANES // chans
    team = n // 2
    chips = team // 2
    me = lax.axis_index("res")
    half = me // team
    seat = lax.rem(me, team)
    core = lax.rem(seat, 2)
    chip = seat // 2
    base = half * team
    partner = (1 - half) * team + seat
    peer_seat = seat + 1 - 2 * core

    def to(dev):
        return dict(device_id={"res": dev}, device_id_type=pl.DeviceIdType.MESH)

    barrier = pltpu.get_barrier_semaphore()

    def greet(k, carry):
        pl.semaphore_signal(barrier, inc=1, **to(base + lax.rem(seat + k, team)))
        return carry

    lax.fori_loop(1, team, greet, 0)
    pl.semaphore_signal(barrier, inc=1, **to(partner))

    def same(shape, down, across):
        r = lax.broadcasted_iota(jnp.int32, shape, 0) // down
        c = lax.broadcasted_iota(jnp.int32, shape, 1) // across
        return r == c

    reps = LANES // width
    lhs = jnp.concatenate([lhs_ref[...].astype(F32)] * per_tile, axis=1)
    lhs = jnp.concatenate([lhs] * reps, axis=0).T
    lhs_wide = jnp.concatenate([lhs] * (reps // per_tile), axis=0)
    lhs_wide = jnp.where(same(lhs_wide.shape, chans, width), lhs_wide, 0.0).astype(BF16)
    fold = width // 2
    rhs = rhs_ref[...].astype(F32)
    rhs_t = jnp.concatenate([rhs[:fold], rhs[fold:]], axis=1).astype(BF16)
    averager = jnp.where(same((LANES, LANES), chans, chans), 1.0 / chans, 0.0).astype(BF16)
    gain = jnp.concatenate([gain_ref[...]] * per_tile, axis=1)
    offset = jnp.concatenate([offset_ref[...]] * per_tile, axis=1)

    group = 8
    dests = group * per_tile // resid
    halves = resid * width // LANES

    def project(b, carry):
        x = jnp.concatenate(
            [
                x_ref[:, pl.ds(pl.multiple_of((b * group + u) * LANES, LANES), LANES)].astype(F32)
                for u in range(group)
            ],
            axis=0,
        )
        center = x - dot(x.astype(BF16), averager)
        square = center * center
        high = square.astype(BF16)
        low = (square - high.astype(F32)).astype(BF16)
        spread = dot(high, averager) + dot(low, averager)
        normed = (center * lax.rsqrt(spread + 1e-05) * gain + offset).astype(BF16)
        wide = normed.astype(F32)
        norm_scr[pl.ds(pl.multiple_of(b * group * rows, 8), group * rows), :] = wide
        even = jnp.concatenate(
            [wide[u * rows : (u + 1) * rows] for u in range(0, group, 2)], axis=0
        ).astype(BF16)
        odd = jnp.concatenate(
            [wide[u * rows : (u + 1) * rows] for u in range(1, group, 2)], axis=0
        ).astype(BF16)
        left = dot(jnp.concatenate([even, odd], axis=1), lhs_wide)
        for u in range(group // 2):
            dest = b * dests + u // halves
            left_send[
                lax.rem(dest, team), dest // team, :, (u % halves) * LANES : (u % halves + 1) * LANES
            ] = left[u * rows : (u + 1) * rows].astype(BF16)
        return carry

    lax.fori_loop(0, tiles // group, project, 0)

    pl.semaphore_wait(barrier, team)

    part = width * residues // WAVES

    def block(at, h):
        return right_all.at[at, :, pl.ds(h * part, part)]

    def right_copy(k, h, incoming):
        other = 2 * lax.rem(chip + k + chips, chips) + core
        ref = block(other if incoming else seat, h)
        slot = chips - k if incoming else k
        return pltpu.make_async_remote_copy(
            src_ref=ref,
            dst_ref=ref,
            send_sem=r_send.at[h, slot],
            recv_sem=r_recv.at[h, slot],
            **to(base + other),
        )

    def share(k, h, theirs):
        source = 2 * lax.rem(chip + k, chips) + (1 - core if theirs else core)
        ref = block(source, h)
        return pltpu.make_async_remote_copy(
            src_ref=ref,
            dst_ref=ref,
            send_sem=peer_send.at[h, k],
            recv_sem=peer_recv.at[h, k],
            **to(base + peer_seat),
        )

    def left_copy(k, incoming):
        slot = team - k if incoming else k
        other = lax.rem(seat + k, team)
        return pltpu.make_async_remote_copy(
            src_ref=left_send.at[other],
            dst_ref=left_all.at[other if incoming else seat],
            send_sem=l_send.at[slot],
            recv_sem=l_recv.at[slot],
            **to(base + other),
        )

    def over(first, last, act):
        def step(k, carry):
            act(k)
            return carry

        lax.fori_loop(first, last, step, 0)

    over(1, team, lambda k: left_copy(k, False).start())

    lane = lax.broadcasted_iota(jnp.int32, (tiles, LANES), 1) // chans
    strips = residues // LANES

    batch = 8

    def turn(b, h):
        ones = [norm_scr[pl.ds(b * batch + v, tiles, stride=rows), :] for v in range(batch)]
        spread_out = jnp.concatenate(
            [
                jnp.where(lane == q, one if q == h else pltpu.roll(one, chans, 1), 0.0)
                for one in ones
                for q in range(2)
            ],
            axis=0,
        ).astype(BF16)
        res = lax.dot_general(
            rhs_t, spread_out, (((1,), (1,)), ((), ())), preferred_element_type=F32
        )
        for v in range(batch):
            for j in range(strips):
                at = v * residues + j * LANES
                turn_scr[h * strips + j, pl.ds(b * batch + v, fold, stride=rows), :] = res[
                    :, at : at + LANES
                ]

    for h in range(WAVES):
        over(0, rows // batch, lambda b: turn(b, h))
        for q in range(fold):
            for j in range(strips):
                at = (h * fold + q) * residues + j * LANES
                right_all[seat, :, at : at + LANES] = turn_scr[
                    h * strips + j, q * rows : (q + 1) * rows, :
                ].astype(BF16)
        over(1, chips, lambda k: right_copy(k, h, False).start())
        share(0, h, False).start()
    left_all[seat] = left_send[seat]

    out_chans = pair_ref.shape[1]
    pair_scr[...] = pair_ref[...].astype(F32)
    for c in range(2):
        for b in range(fold // reps):
            some = jnp.concatenate(
                [
                    pair_scr[pl.ds(c * fold + b * reps + u, width, stride=width), :]
                    for u in range(reps)
                ],
                axis=0,
            )
            pair_t[c * out_chans : (c + 1) * out_chans, b * LANES : (b + 1) * LANES] = (
                some.T.astype(BF16)
            )

    def gather(h):
        def pass_on(k):
            right_copy(k, h, True).wait_recv()
            share(k, h, False).start()

        over(1, chips, pass_on)

    def gathered(h):
        over(0, chips, lambda k: share(k, h, True).wait_recv())

    qs = 4
    here_rows = team * rows
    total = n * rows
    first = lax.broadcasted_iota(jnp.int32, (out_chans, residues), 1) < tiles

    def fill(which, h):
        def outer(b):
            here = right_all[
                :,
                :,
                pl.ds(
                    pl.multiple_of(h * fold * residues + b * qs * residues, LANES), qs * residues
                ),
            ]
            if rows % 16:
                here = here.astype(F32)
            here = here.reshape(here_rows, qs * residues).astype(BF16)
            product = (dot(left_t[which], here) * (1.0 / total)).astype(BF16)
            for u in range(qs):
                for i in range(resid):
                    flat[
                        pl.ds(pl.multiple_of((b * qs + u) * width, width), width),
                        i * residues : (i + 1) * residues,
                    ] = product[i * width : (i + 1) * width, u * residues : (u + 1) * residues]

        over(0, fold // qs, outer)

    def sums(b, h):
        return pltpu.make_async_remote_copy(
            src_ref=sum_send.at[h, b],
            dst_ref=sum_recv.at[h, b],
            send_sem=s_send.at[h, b],
            recv_sem=s_recv.at[h, b],
            **to(partner),
        )

    def mapped(b):
        both = dot(pair_t[...], flat[:, b * 2 * residues : (b + 1) * 2 * residues])
        low, high = both[:out_chans], both[out_chans:]
        one = low[:, :residues] + pltpu.roll(high[:, :residues], tiles, 1)
        two = pltpu.roll(low[:, residues:], tiles, 1) + high[:, residues:]
        return jnp.where(first, one, two)

    def theirs(h):
        fill(1 - half, h)
        for b in range(resid // 2):
            sum_send[h, b] = mapped(b).astype(BF16)
            sums(b, h).start()

    def mine(h):
        fill(half, h)
        for b in range(resid // 2):
            kept[h, b] = mapped(b)

    def finish(h):
        for b in range(resid // 2):
            sums(b, h).wait_recv()
            turned = (kept[h, b] + sum_recv[h, b].astype(F32)).T + shift_ref[...]
            for u in range(2):
                mix[2 * b + u, pl.ds(h, tiles, stride=2), :] = turned[u * tiles : (u + 1) * tiles]

    gather(0)
    over(1, team, lambda k: left_copy(k, True).wait_recv())
    for b in range(2):
        left_t[b] = (
            left_all[:, b].astype(F32).reshape(team * rows, resid * width).T.astype(BF16)
        )
    gathered(0)
    theirs(0)
    gather(1)
    mine(0)
    gathered(1)
    theirs(1)
    mine(1)
    finish(0)
    finish(1)
    for i in range(resid):
        out_ref[i] = mix[i].astype(BF16)

    for h in range(WAVES):
        over(1, chips, lambda k: right_copy(k, h, False).wait_send())
        over(0, chips, lambda k: share(k, h, False).wait_send())
    over(1, team, lambda k: left_copy(k, False).wait_send())
    for h in range(WAVES):
        for b in range(resid // 2):
            sums(b, h).wait_send()


def on_device(n, x, gain, offset, lhs, rhs, pair, shift):
    rows = x.shape[0]
    chans, width = lhs.shape
    residues = x.shape[1] // chans
    resid = residues // n
    tiles = x.shape[1] // LANES
    team = n // 2
    chips = team // 2
    depth = width * width
    out_chans = pair.shape[1]
    vmem = pl.BlockSpec(memory_space=pltpu.VMEM)
    return pl.pallas_call(
        functools.partial(kernel, n),
        out_shape=jax.ShapeDtypeStruct((resid, residues, out_chans), BF16),
        in_specs=[vmem] * 7,
        out_specs=vmem,
        scratch_shapes=[
            pltpu.VMEM((tiles * rows, LANES), F32),
            pltpu.VMEM((2 * residues // LANES, width // 2 * rows, LANES), F32),
            pltpu.VMEM((depth, out_chans), F32),
            pltpu.VMEM((2 * out_chans, depth // 2), BF16),
            pltpu.VMEM((team, 2, rows, resid * width), BF16),
            pltpu.VMEM((team, 2, rows, resid * width), BF16),
            pltpu.VMEM((2, resid * width, team * rows), BF16),
            pltpu.VMEM((team, rows, width * residues), BF16),
            pltpu.VMEM((depth // 2, resid * residues), BF16),
            pltpu.VMEM((resid, residues, out_chans), F32),
            pltpu.VMEM((WAVES, resid // 2, out_chans, residues), F32),
            pltpu.VMEM((WAVES, resid // 2, out_chans, residues), BF16),
            pltpu.VMEM((WAVES, resid // 2, out_chans, residues), BF16),
            pltpu.SemaphoreType.DMA((team,)),
            pltpu.SemaphoreType.DMA((team,)),
            pltpu.SemaphoreType.DMA((WAVES, chips)),
            pltpu.SemaphoreType.DMA((WAVES, chips)),
            pltpu.SemaphoreType.DMA((WAVES, chips)),
            pltpu.SemaphoreType.DMA((WAVES, chips)),
            pltpu.SemaphoreType.DMA((WAVES, resid // 2)),
            pltpu.SemaphoreType.DMA((WAVES, resid // 2)),
        ],
        compiler_params=pltpu.CompilerParams(
            collective_id=0, has_side_effects=True, vmem_limit_bytes=56 * 1024 * 1024
        ),
    )(x, gain.reshape(1, -1), offset.reshape(1, -1), lhs.T, rhs.T, pair, shift.reshape(1, -1))


def solution(mesh):
    in_specs = (P(("grp", "res"), None), P(), P(), P(), P(), P(), P())
    out_specs = P(("grp", "res"), None, None)
    return jax.shard_map(
        functools.partial(on_device, mesh.shape["res"]),
        mesh=mesh,
        in_specs=in_specs,
        out_specs=out_specs,
        check_vma=False,
    )
```

```python
import functools

import jax
import jax.numpy as jnp
from jax import lax
from jax.experimental import pallas as pl
from jax.experimental.pallas import tpu as pltpu
from jax.sharding import PartitionSpec as P

F32 = jnp.float32
BF16 = jnp.bfloat16
LANES = 128
WAVES = 2


def dot(a, b):
    return jnp.dot(a, b, preferred_element_type=F32)


def kernel(
    n,
    x_ref,
    gain_ref,
    offset_ref,
    lhs_ref,
    rhs_ref,
    pair_ref,
    shift_ref,
    out_ref,
    norm_scr,
    turn_scr,
    pair_scr,
    pair_t,
    left_send,
    left_all,
    left_t,
    right_all,
    flat,
    mix,
    kept,
    sum_send,
    sum_recv,
    l_send,
    l_recv,
    r_send,
    r_recv,
    peer_send,
    peer_recv,
    s_send,
    s_recv,
):
    rows = x_ref.shape[0]
    width, chans = lhs_ref.shape
    residues = x_ref.shape[1] // chans
    resid = residues // n
    tiles = x_ref.shape[1] // LANES
    per_tile = LANES // chans
    team = n // 2
    chips = team // 2
    me = lax.axis_index("res")
    half = me // team
    seat = lax.rem(me, team)
    core = lax.rem(seat, 2)
    chip = seat // 2
    base = half * team
    partner = (1 - half) * team + seat
    peer_seat = seat + 1 - 2 * core

    def to(dev):
        return dict(device_id={"res": dev}, device_id_type=pl.DeviceIdType.MESH)

    barrier = pltpu.get_barrier_semaphore()

    def greet(k, carry):
        pl.semaphore_signal(barrier, inc=1, **to(base + lax.rem(seat + k, team)))
        return carry

    lax.fori_loop(1, team, greet, 0)
    pl.semaphore_signal(barrier, inc=1, **to(partner))

    def same(shape, down, across):
        r = lax.broadcasted_iota(jnp.int32, shape, 0) // down
        c = lax.broadcasted_iota(jnp.int32, shape, 1) // across
        return r == c

    reps = LANES // width
    lhs = jnp.concatenate([lhs_ref[...].astype(F32)] * per_tile, axis=1)
    lhs = jnp.concatenate([lhs] * reps, axis=0).T
    lhs_wide = jnp.concatenate([lhs] * (reps // per_tile), axis=0)
    lhs_wide = jnp.where(same(lhs_wide.shape, chans, width), lhs_wide, 0.0).astype(BF16)
    fold = width // 2
    rhs = rhs_ref[...].astype(F32)
    rhs_t = jnp.concatenate([rhs[:fold], rhs[fold:]], axis=1).astype(BF16)
    averager = jnp.where(same((LANES, LANES), chans, chans), 1.0 / chans, 0.0).astype(BF16)
    gain = jnp.concatenate([gain_ref[...]] * per_tile, axis=1)
    offset = jnp.concatenate([offset_ref[...]] * per_tile, axis=1)

    group = 8
    dests = group * per_tile // resid
    halves = resid * width // LANES

    def project(b, carry):
        x = jnp.concatenate(
            [
                x_ref[:, pl.ds(pl.multiple_of((b * group + u) * LANES, LANES), LANES)].astype(F32)
                for u in range(group)
            ],
            axis=0,
        )
        center = x - dot(x.astype(BF16), averager)
        square = center * center
        high = square.astype(BF16)
        low = (square - high.astype(F32)).astype(BF16)
        spread = dot(high, averager) + dot(low, averager)
        normed = (center * lax.rsqrt(spread + 1e-05) * gain + offset).astype(BF16)
        wide = normed.astype(F32)
        norm_scr[pl.ds(pl.multiple_of(b * group * rows, 8), group * rows), :] = wide
        even = jnp.concatenate(
            [wide[u * rows : (u + 1) * rows] for u in range(0, group, 2)], axis=0
        ).astype(BF16)
        odd = jnp.concatenate(
            [wide[u * rows : (u + 1) * rows] for u in range(1, group, 2)], axis=0
        ).astype(BF16)
        left = dot(jnp.concatenate([even, odd], axis=1), lhs_wide)
        for u in range(group // 2):
            dest = b * dests + u // halves
            left_send[
                lax.rem(dest, team), dest // team, :, (u % halves) * LANES : (u % halves + 1) * LANES
            ] = left[u * rows : (u + 1) * rows].astype(BF16)
        return carry

    lax.fori_loop(0, tiles // group, project, 0)

    pl.semaphore_wait(barrier, team)

    part = width * residues // WAVES

    def block(at, h):
        return right_all.at[at, :, pl.ds(h * part, part)]

    def right_copy(k, h, incoming):
        other = 2 * lax.rem(chip + k + chips, chips) + core
        ref = block(other if incoming else seat, h)
        slot = chips - k if incoming else k
        return pltpu.make_async_remote_copy(
            src_ref=ref,
            dst_ref=ref,
            send_sem=r_send.at[h, slot],
            recv_sem=r_recv.at[h, slot],
            **to(base + other),
        )

    def share(k, h, theirs):
        source = 2 * lax.rem(chip + k, chips) + (1 - core if theirs else core)
        ref = block(source, h)
        return pltpu.make_async_remote_copy(
            src_ref=ref,
            dst_ref=ref,
            send_sem=peer_send.at[h, k],
            recv_sem=peer_recv.at[h, k],
            **to(base + peer_seat),
        )

    def left_copy(k, incoming):
        slot = team - k if incoming else k
        other = lax.rem(seat + k, team)
        return pltpu.make_async_remote_copy(
            src_ref=left_send.at[other],
            dst_ref=left_all.at[other if incoming else seat],
            send_sem=l_send.at[slot],
            recv_sem=l_recv.at[slot],
            **to(base + other),
        )

    def over(first, last, act):
        def step(k, carry):
            act(k)
            return carry

        lax.fori_loop(first, last, step, 0)

    over(1, team, lambda k: left_copy(k, False).start())

    lane = lax.broadcasted_iota(jnp.int32, (tiles, LANES), 1) // chans
    strips = residues // LANES

    batch = 8

    def turn(b, h):
        ones = [norm_scr[pl.ds(b * batch + v, tiles, stride=rows), :] for v in range(batch)]
        spread_out = jnp.concatenate(
            [
                jnp.where(lane == q, one if q == h else pltpu.roll(one, chans, 1), 0.0)
                for one in ones
                for q in range(2)
            ],
            axis=0,
        ).astype(BF16)
        res = lax.dot_general(
            rhs_t, spread_out, (((1,), (1,)), ((), ())), preferred_element_type=F32
        )
        for v in range(batch):
            for j in range(strips):
                at = v * residues + j * LANES
                turn_scr[h * strips + j, pl.ds(b * batch + v, fold, stride=rows), :] = res[
                    :, at : at + LANES
                ]

    for h in range(WAVES):
        over(0, rows // batch, lambda b: turn(b, h))
        for q in range(fold):
            for j in range(strips):
                at = (h * fold + q) * residues + j * LANES
                right_all[seat, :, at : at + LANES] = turn_scr[
                    h * strips + j, q * rows : (q + 1) * rows, :
                ].astype(BF16)
        over(1, chips, lambda k: right_copy(k, h, False).start())
        share(0, h, False).start()
    left_all[seat] = left_send[seat]

    out_chans = pair_ref.shape[1]
    pair_scr[...] = pair_ref[...].astype(F32)
    for c in range(2):
        for b in range(fold // reps):
            some = jnp.concatenate(
                [
                    pair_scr[pl.ds(c * fold + b * reps + u, width, stride=width), :]
                    for u in range(reps)
                ],
                axis=0,
            )
            pair_t[c * out_chans : (c + 1) * out_chans, b * LANES : (b + 1) * LANES] = (
                some.T.astype(BF16)
            )

    def gather(h):
        def pass_on(k):
            right_copy(k, h, True).wait_recv()
            share(k, h, False).start()

        over(1, chips, pass_on)

    def gathered(h):
        over(0, chips, lambda k: share(k, h, True).wait_recv())

    qs = 4
    here_rows = team * rows
    total = n * rows
    first = lax.broadcasted_iota(jnp.int32, (out_chans, residues), 1) < tiles

    def fill(which, h):
        def outer(b):
            here = right_all[
                :,
                :,
                pl.ds(
                    pl.multiple_of(h * fold * residues + b * qs * residues, LANES), qs * residues
                ),
            ]
            if rows % 16:
                here = here.astype(F32)
            here = here.reshape(here_rows, qs * residues).astype(BF16)
            product = (dot(left_t[which], here) * (1.0 / total)).astype(BF16)
            for u in range(qs):
                for i in range(resid):
                    flat[
                        pl.ds(pl.multiple_of((b * qs + u) * width, width), width),
                        i * residues : (i + 1) * residues,
                    ] = product[i * width : (i + 1) * width, u * residues : (u + 1) * residues]

        for b in range(fold // qs):
            outer(b)

    def sums(b, h):
        return pltpu.make_async_remote_copy(
            src_ref=sum_send.at[h, b],
            dst_ref=sum_recv.at[h, b],
            send_sem=s_send.at[h, b],
            recv_sem=s_recv.at[h, b],
            **to(partner),
        )

    def mapped(b):
        both = dot(pair_t[...], flat[:, b * 2 * residues : (b + 1) * 2 * residues])
        low, high = both[:out_chans], both[out_chans:]
        one = low[:, :residues] + pltpu.roll(high[:, :residues], tiles, 1)
        two = pltpu.roll(low[:, residues:], tiles, 1) + high[:, residues:]
        return jnp.where(first, one, two)

    def theirs(h):
        fill(1 - half, h)
        for b in range(resid // 2):
            sum_send[h, b] = mapped(b).astype(BF16)
            sums(b, h).start()

    def mine(h):
        fill(half, h)
        for b in range(resid // 2):
            kept[h, b] = mapped(b)

    def finish(h):
        for b in range(resid // 2):
            sums(b, h).wait_recv()
            turned = (kept[h, b] + sum_recv[h, b].astype(F32)).T + shift_ref[...]
            for u in range(2):
                mix[2 * b + u, pl.ds(h, tiles, stride=2), :] = turned[u * tiles : (u + 1) * tiles]

    gather(0)
    over(1, team, lambda k: left_copy(k, True).wait_recv())
    for b in range(2):
        left_t[b] = (
            left_all[:, b].astype(F32).reshape(team * rows, resid * width).T.astype(BF16)
        )
    gathered(0)
    theirs(0)
    gather(1)
    mine(0)
    gathered(1)
    theirs(1)
    mine(1)
    finish(0)
    finish(1)
    for i in range(resid):
        out_ref[i] = mix[i].astype(BF16)

    for h in range(WAVES):
        over(1, chips, lambda k: right_copy(k, h, False).wait_send())
        over(0, chips, lambda k: share(k, h, False).wait_send())
    over(1, team, lambda k: left_copy(k, False).wait_send())
    for h in range(WAVES):
        for b in range(resid // 2):
            sums(b, h).wait_send()


def on_device(n, x, gain, offset, lhs, rhs, pair, shift):
    rows = x.shape[0]
    chans, width = lhs.shape
    residues = x.shape[1] // chans
    resid = residues // n
    tiles = x.shape[1] // LANES
    team = n // 2
    chips = team // 2
    depth = width * width
    out_chans = pair.shape[1]
    vmem = pl.BlockSpec(memory_space=pltpu.VMEM)
    return pl.pallas_call(
        functools.partial(kernel, n),
        out_shape=jax.ShapeDtypeStruct((resid, residues, out_chans), BF16),
        in_specs=[vmem] * 7,
        out_specs=vmem,
        scratch_shapes=[
            pltpu.VMEM((tiles * rows, LANES), F32),
            pltpu.VMEM((2 * residues // LANES, width // 2 * rows, LANES), F32),
            pltpu.VMEM((depth, out_chans), F32),
            pltpu.VMEM((2 * out_chans, depth // 2), BF16),
            pltpu.VMEM((team, 2, rows, resid * width), BF16),
            pltpu.VMEM((team, 2, rows, resid * width), BF16),
            pltpu.VMEM((2, resid * width, team * rows), BF16),
            pltpu.VMEM((team, rows, width * residues), BF16),
            pltpu.VMEM((depth // 2, resid * residues), BF16),
            pltpu.VMEM((resid, residues, out_chans), F32),
            pltpu.VMEM((WAVES, resid // 2, out_chans, residues), F32),
            pltpu.VMEM((WAVES, resid // 2, out_chans, residues), BF16),
            pltpu.VMEM((WAVES, resid // 2, out_chans, residues), BF16),
            pltpu.SemaphoreType.DMA((team,)),
            pltpu.SemaphoreType.DMA((team,)),
            pltpu.SemaphoreType.DMA((WAVES, chips)),
            pltpu.SemaphoreType.DMA((WAVES, chips)),
            pltpu.SemaphoreType.DMA((WAVES, chips)),
            pltpu.SemaphoreType.DMA((WAVES, chips)),
            pltpu.SemaphoreType.DMA((WAVES, resid // 2)),
            pltpu.SemaphoreType.DMA((WAVES, resid // 2)),
        ],
        compiler_params=pltpu.CompilerParams(
            collective_id=0, has_side_effects=True, vmem_limit_bytes=56 * 1024 * 1024
        ),
    )(x, gain.reshape(1, -1), offset.reshape(1, -1), lhs.T, rhs.T, pair, shift.reshape(1, -1))


def solution(mesh):
    in_specs = (P(("grp", "res"), None), P(), P(), P(), P(), P(), P())
    out_specs = P(("grp", "res"), None, None)
    return jax.shard_map(
        functools.partial(on_device, mesh.shape["res"]),
        mesh=mesh,
        in_specs=in_specs,
        out_specs=out_specs,
        check_vma=False,
    )
```
